256 devices in a mesh: section: 4 (over z_lo, core), seq: 16 (over x, y), dp: 4 (over z_hi).
Axes of the slice: x: 4, y: 4, z: 8 (z_hi: 4, z_lo: 2; z = z_hi * 2 + z_lo), core: 2. Of those that a mesh axis runs over, the one named last changes fastest.
Arguments:
- act_rows: bfloat16 [4, 4, 1024, 4096], P('section', 'dp', 'seq'), may hold values from -30 to 30
- mem_rows: bfloat16 [4, 4, 1024, 4096], P('section', 'dp', 'seq'), may hold values from -30 to 30
- w_query: bfloat16 [4, 4096, 4096], P('section', 'dp', 'seq'), may hold values from -8 to 8
- w_key: bfloat16 [4, 4096, 4096], P('section', 'dp', 'seq'), may hold values from -8 to 8
- w_value: bfloat16 [4, 4096, 4096], P('section', 'dp', 'seq'), may hold values from -0.09375 to 0.09375
- w_out: bfloat16 [4, 4096, 4096], P('section', ('seq', 'dp')), may hold values from -0.09375 to 0.09375
- ln_gain: float32 [4, 4096], P('section'), may hold values from 0.5 to 1.5
- final_gain: float32 [4096], replicated, may hold values from 0.5 to 1.5
- src_len: int32 [4, 4], P('section', 'dp'), may hold values from 256 to 1024
- tgt_len: int32 [4, 4], P('section', 'dp'), may hold values from 256 to 1024
Outputs:
- act_next: bfloat16 [4, 4, 1024, 4096], P('section', 'dp', 'seq')
- mem_next: bfloat16 [4, 4, 1024, 4096], P('section', 'dp', 'seq')
The draws below stay inside these ranges and needn't reach their ends.
All inputs are finite; a program needn't handle non-finite values.
Results may differ from the reference program's by a relative error of at most 0.013.
The reference program's roundings to bfloat16 on the way count: a program that leaves them out, or rounds other values in their place, can miss the bound.
Values may be sent and summed in bfloat16 or wider, within the bound.
No kernel may reach another device: no remote copies, remote signals or barrier semaphores. Data moves between devices by JAX's collectives and lax.ppermute only.
A program may use at most 128 MiB of HBM per device.

```python
import math
import jax
import jax.numpy as jnp
from jax import lax

D = 4096
HEADS = 64
HEAD_DIM = 64
SEQ_LEN = 1024
SEQS = 4
SECTIONS = 4
N_SEQ = 16


def row_scales(key, shape):
    return jnp.exp(jax.random.uniform(key, shape, jnp.float32, math.log(0.3), math.log(3.0)))


def memory_base(key):
    shape = (SECTIONS, SEQS, SEQ_LEN, D)
    return jnp.clip(jax.random.normal(jax.random.fold_in(key, 201), shape, jnp.float32), -5.0, 5.0)


def draw_mem_rows(key, part):
    values = memory_base(key) * row_scales(jax.random.fold_in(key, 211), (SECTIONS, SEQS, SEQ_LEN, 1))
    return values.astype(jnp.bfloat16)


def draw_act_rows(key, part):
    shape = (SECTIONS, SEQS, SEQ_LEN, D)
    own_part = jnp.clip(jax.random.normal(jax.random.fold_in(key, 202), shape, jnp.float32), -5.0, 5.0)
    values = own_part * row_scales(jax.random.fold_in(key, 212), (SECTIONS, SEQS, SEQ_LEN, 1))
    return values.astype(jnp.bfloat16)


def query_base(key):
    shape = (SECTIONS, D, HEADS * HEAD_DIM)
    return jnp.clip(jax.random.normal(jax.random.fold_in(key, 301), shape, jnp.float32), -6.0, 6.0)


def draw_w_query(key, part):
    values = query_base(key) * (1.0 / math.sqrt(D))
    return values.astype(jnp.bfloat16)


def draw_w_key(key, part):
    shape = (SECTIONS, D, HEADS * HEAD_DIM)
    own_part = jnp.clip(jax.random.normal(jax.random.fold_in(key, 302), shape, jnp.float32), -6.0, 6.0)
    values = own_part * (1.0 / math.sqrt(D))
    return values.astype(jnp.bfloat16)


def with_ends(array, key, smallest, high):
    index_at = [jax.random.randint(jax.random.fold_in(key, axis), (), 0, length) for axis, length in enumerate(array.shape)]
    main_axis = array.shape.index(max(array.shape))
    neighbour = index_at[:main_axis] + [(index_at[main_axis] + 1) % array.shape[main_axis]] + index_at[main_axis + 1:]
    return array.at[tuple(index_at)].set(smallest).at[tuple(neighbour)].set(high)


def block_scale(stream_key, extent, cuts, least, high):
    level, own = 1.0, jax.random.fold_in(stream_key, 6)
    for dim, shards_of in cuts:
        heights = jnp.exp(jax.random.uniform(jax.random.fold_in(own, dim), (shards_of,), jnp.float32, least / len(cuts), high / len(cuts)))
        level = level * jnp.repeat(heights, extent[dim] // shards_of).reshape([-1 if axis == dim else 1 for axis in range(len(extent))])
    return level


def normal_values(rng, dims, spread, bound, shards=(), held_as=jnp.bfloat16):
    loudness = block_scale(rng, dims, shards, -0.22, 0.18) if shards else 1.0
    result = jax.random.normal(rng, dims, jnp.float32) * spread * loudness
    return jnp.minimum(jnp.maximum(result, -bound), bound).astype(held_as)


def setup_inputs(seed: int = 0) -> dict:
    seeds = jax.random.split(jax.random.key(seed), 11)
    act_rows = draw_act_rows(jax.random.fold_in(seeds[10], 71), 0)
    mem_rows = draw_mem_rows(jax.random.fold_in(seeds[10], 71), 0)
    w_query = draw_w_query(jax.random.fold_in(seeds[10], 71), 0)
    w_key = draw_w_key(jax.random.fold_in(seeds[10], 71), 0)
    w_value = normal_values(seeds[4], (SECTIONS, D, HEADS * HEAD_DIM), D ** -0.5, 0.09375, ((0, 4), (1, 4), (2, 16)))
    w_out = normal_values(seeds[5], (SECTIONS, HEADS * HEAD_DIM, D), (HEADS * HEAD_DIM) ** -0.5, 0.09375, ((0, 4), (1, 64)))
    ln_gain = jnp.clip(1.0 + 0.1 * jax.random.normal(seeds[6], (SECTIONS, D), jnp.float32), 0.5, 1.5)
    final_gain = jnp.clip(1.0 + 0.1 * jax.random.normal(seeds[7], (D,), jnp.float32), 0.5, 1.5)
    src_len = with_ends(jax.random.randint(seeds[8], (SECTIONS, SEQS), SEQ_LEN // 4, SEQ_LEN + 1), jax.random.fold_in(seeds[8], 1), SEQ_LEN // 4, SEQ_LEN).astype(jnp.int32)
    tgt_len = with_ends(jax.random.randint(seeds[9], (SECTIONS, SEQS), SEQ_LEN // 4, SEQ_LEN + 1), jax.random.fold_in(seeds[9], 1), SEQ_LEN // 4, SEQ_LEN).astype(jnp.int32)
    return {"act_rows": act_rows, "mem_rows": mem_rows, "w_query": w_query, "w_key": w_key, "w_value": w_value, "w_out": w_out, "ln_gain": ln_gain, "final_gain": final_gain, "src_len": src_len, "tgt_len": tgt_len}


EPS = 1e-06

def normed(rows, gain):
    values = rows.astype(jnp.float32)
    scaled = values * lax.rsqrt(lax.optimization_barrier(jnp.mean(values * values, axis=-1, keepdims=True)) + EPS)
    return (scaled * gain).astype(jnp.bfloat16)

def attend(query, key, value, src_length):
    total_rows = query.shape[0]
    query_heads = query.astype(jnp.float32).reshape(total_rows, HEADS, HEAD_DIM)
    key_heads = key.astype(jnp.float32).reshape(total_rows, HEADS, HEAD_DIM)
    value_heads = value.astype(jnp.float32).reshape(total_rows, HEADS, HEAD_DIM)
    scores = jnp.einsum('qhd,khd->hqk', query_heads, key_heads) * HEAD_DIM ** (-0.5)
    visible = jnp.arange(total_rows, dtype=jnp.int32) < src_length
    scores = jnp.where(visible[None, None, :], scores, -1e+30)
    top_score = lax.optimization_barrier(jnp.max(scores, axis=-1, keepdims=True))
    raw_weights = jnp.exp(scores - top_score)
    weights = (raw_weights / lax.optimization_barrier(jnp.sum(raw_weights, axis=-1, keepdims=True))).astype(jnp.bfloat16)
    heads_out = jnp.einsum('hqk,khd->qhd', weights.astype(jnp.float32), value_heads)
    return heads_out.astype(jnp.bfloat16).reshape(total_rows, HEADS * HEAD_DIM)

def reference(act_rows, mem_rows, w_query, w_key, w_value, w_out, ln_gain, final_gain, src_len, tgt_len):
    width = HEADS * HEAD_DIM
    group_cols = width // N_SEQ
    emit_act = []
    emit_mem = []
    for section in range(SECTIONS):
        act_list = []
        mem_list = []
        for sequence in range(SEQS):
            if section == 0:
                rows_in = mem_rows[0, sequence]
            else:
                rows_in = act_rows[section, sequence]
            residual = rows_in.astype(jnp.float32)
            query_in = normed(rows_in, ln_gain[section])
            if section == 0:
                source_in = query_in
            else:
                source_in = mem_rows[section, sequence]
            query = jnp.dot(query_in, w_query[section], preferred_element_type=jnp.float32).astype(jnp.bfloat16)
            key = jnp.dot(source_in, w_key[section], preferred_element_type=jnp.float32).astype(jnp.bfloat16)
            value = jnp.dot(source_in, w_value[section], preferred_element_type=jnp.float32).astype(jnp.bfloat16)
            heads_out = attend(query, key, value, src_len[section, sequence])
            update = jnp.zeros((SEQ_LEN, D), jnp.float32)
            for group in range(N_SEQ):
                low = group * group_cols
                high = low + group_cols
                partial_sum = jnp.dot(heads_out[:, low:high], w_out[section, low:high, :], preferred_element_type=jnp.float32).astype(jnp.bfloat16)
                partial_sum = lax.optimization_barrier(partial_sum)
                update = update + partial_sum.astype(jnp.float32)
            if section == 0:
                encoded = normed(residual + update, final_gain)
                act_list.append(act_rows[0, sequence])
                mem_list.append(encoded)
            else:
                positions = jnp.arange(SEQ_LEN, dtype=jnp.int32)
                keep_rows = (positions < tgt_len[section, sequence])[:, None]
                decoded = (residual + jnp.where(keep_rows, update, jnp.float32(0.0))).astype(jnp.bfloat16)
                act_list.append(decoded)
                mem_list.append(mem_rows[section, sequence])
        emit_act.append(jnp.stack(act_list))
        emit_mem.append(jnp.stack(mem_list))
    order = [SECTIONS - 1] + list(range(SECTIONS - 1))
    act_next = jnp.stack([emit_act[k] for k in order])
    mem_next = jnp.stack([emit_mem[k] for k in order])
    return (act_next, mem_next)
```

```python
import jax
import jax.numpy as jnp
from jax import lax
from jax.sharding import PartitionSpec as P

HEAD_DIM = 64
EPS = 1e-06
SIDE = 4

STEPS = (0, -1, 1, 2)


def along_section(x):
    return lax.ppermute(x, "section", [(i, (i + 1) % 4) for i in range(4)])


def along_dp(x, by):
    return lax.ppermute(x, "dp", [(i, (i + by) % SIDE) for i in range(SIDE)])


def along_x(x, by):
    pairs = [(a * SIDE + b, (a + by) % SIDE * SIDE + b) for a in range(SIDE) for b in range(SIDE)]
    return lax.ppermute(x, "seq", pairs)


def along_y(x, by):
    pairs = [(a * SIDE + b, a * SIDE + (b + by) % SIDE) for a in range(SIDE) for b in range(SIDE)]
    return lax.ppermute(x, "seq", pairs)


def ring_pieces(x, move):
    half = x.shape[0] // 2
    back = move(x, 1)
    ahead = move(x, -1)
    opposite_low = move(back[:half], 1)
    opposite_high = move(ahead[half:], -1)
    return x, back, ahead, opposite_low, opposite_high


def ring_gather(x, move):
    return jnp.concatenate(ring_pieces(x, move), axis=0)


def ring_gather_ordered(x, move, me):
    rows = x.shape[0]
    own, back, ahead, low, high = ring_pieces(x, move)
    whole = jnp.zeros((SIDE * rows,) + x.shape[1:], x.dtype)
    places = [
        (own, me % SIDE * rows),
        (back, (me + 3) % SIDE * rows),
        (ahead, (me + 1) % SIDE * rows),
        (low, (me + 2) % SIDE * rows),
        (high, (me + 2) % SIDE * rows + rows // 2),
    ]
    for piece, start in places:
        whole = lax.dynamic_update_slice_in_dim(whole, piece, start, axis=0)
    return whole


def added(a, b):
    return (a.astype(jnp.float32) + b.astype(jnp.float32)).astype(a.dtype)


def ring_scatter(chunks, move):
    own, to_back, to_ahead, opposite = chunks
    half = own.shape[0] // 2
    from_back = move(opposite[:half], 1)
    from_ahead = move(opposite[half:], -1)
    to_ahead = jnp.concatenate([added(to_ahead[:half], from_back), to_ahead[half:]], axis=0)
    to_back = jnp.concatenate([to_back[:half], added(to_back[half:], from_ahead)], axis=0)
    one = move(to_ahead, 1)
    other = move(to_back, -1)
    return own.astype(jnp.float32) + one.astype(jnp.float32) + other.astype(jnp.float32)


def normed(rows, gain):
    values = rows.astype(jnp.float32)
    scaled = values * lax.rsqrt(jnp.mean(values * values, axis=-1, keepdims=True) + EPS)
    return (scaled * gain).astype(jnp.bfloat16)


def attend(queries, keys_values, visible):
    total_rows, width = queries.shape
    head_count = width // HEAD_DIM
    keys = keys_values[:, :width].reshape(total_rows, head_count, HEAD_DIM)
    values = keys_values[:, width:].reshape(total_rows, head_count, HEAD_DIM)
    block_rows = min(512, total_rows)
    blocks = queries.reshape(total_rows // block_rows, block_rows, head_count, HEAD_DIM)

    def one_block(query_block):
        scores = jnp.einsum(
            "qhd,khd->hqk", query_block, keys, preferred_element_type=jnp.float32
        ) * HEAD_DIM ** (-0.5)
        scores = jnp.where(visible[None, None, :], scores, -1e30)
        top_score = jnp.max(scores, axis=-1, keepdims=True)
        raw_weights = jnp.exp(scores - top_score)
        weights = (raw_weights / jnp.sum(raw_weights, axis=-1, keepdims=True)).astype(jnp.bfloat16)
        return jnp.einsum(
            "hqk,khd->qhd", weights, values, preferred_element_type=jnp.float32
        ).astype(jnp.bfloat16)

    return lax.map(one_block, blocks).reshape(total_rows, width)


def per_device(
    act_rows, mem_rows, w_query, w_key, w_value, w_out, ln_gain, final_gain, src_len, tgt_len
):
    section = lax.axis_index("section")
    is_first = section == 0
    dp = lax.axis_index("dp")
    place = lax.axis_index("seq")
    place_x = place // SIDE
    place_y = place % SIDE
    act_here = act_rows[0, 0]
    mem_here = mem_rows[0, 0]
    rows_here, model = act_here.shape
    heads_here = w_query.shape[2]

    rows_in = jnp.where(is_first, mem_here, act_here)
    query_in = normed(rows_in, ln_gain[0])
    source_in = jnp.where(is_first, query_in, mem_here)

    pair_cols = ring_gather_ordered(jnp.concatenate([w_key[0], w_value[0]], axis=1), along_dp, dp)
    query_cols = ring_gather_ordered(w_query[0], along_dp, dp)
    out_rows = ring_gather_ordered(w_out[0], along_dp, dp)
    all_queries_in = ring_gather(ring_gather(query_in, along_x), along_y)
    all_sources_in = ring_gather(ring_gather(source_in, along_y), along_x)

    steps = jnp.array(STEPS, jnp.int32)
    source_places = ((place_x + steps) % SIDE)[:, None] * SIDE + ((place_y + steps) % SIDE)[None, :]
    key_positions = (
        source_places[:, :, None] * rows_here + jnp.arange(rows_here, dtype=jnp.int32)
    ).reshape(-1)
    visible = key_positions < src_len[0, 0]

    keys_values = jnp.dot(
        all_sources_in, pair_cols, preferred_element_type=jnp.float32
    ).astype(jnp.bfloat16)
    queries = jnp.dot(
        all_queries_in, query_cols, preferred_element_type=jnp.float32
    ).astype(jnp.bfloat16)
    heads_out = attend(queries, keys_values, visible)
    products = jnp.dot(heads_out, out_rows, preferred_element_type=jnp.float32).astype(jnp.bfloat16)
    products = products.reshape(SIDE, SIDE, rows_here, model)
    mid = model // 2
    first = ring_scatter([products[j, :, :, :mid] for j in range(SIDE)], along_y)
    first = first.astype(jnp.bfloat16)
    first = ring_scatter([first[j] for j in range(SIDE)], along_x)
    second = ring_scatter([products[:, j, :, mid:] for j in range(SIDE)], along_x)
    second = second.astype(jnp.bfloat16)
    second = ring_scatter([second[j] for j in range(SIDE)], along_y)
    update = jnp.concatenate([first, second], axis=1)

    residual = rows_in.astype(jnp.float32)
    positions = place * rows_here + jnp.arange(rows_here, dtype=jnp.int32)
    keep_rows = (positions < tgt_len[0, 0])[:, None]
    decoded = (residual + jnp.where(keep_rows, update, jnp.float32(0.0))).astype(jnp.bfloat16)
    encoded = normed(residual + update, final_gain)
    fresh = along_section(jnp.where(is_first, encoded, decoded))
    passed = along_section(jnp.where(is_first, act_here, mem_here))
    after_first = section == 1
    next_act = jnp.where(after_first, passed, fresh)
    next_mem = jnp.where(after_first, fresh, passed)
    return (next_act[None, None], next_mem[None, None])


def solution(mesh):
    return jax.shard_map(
        per_device,
        mesh=mesh,
        in_specs=(
            P("section", "dp", "seq", None),
            P("section", "dp", "seq", None),
            P("section", "dp", "seq"),
            P("section", "dp", "seq"),
            P("section", "dp", "seq"),
            P("section", ("seq", "dp"), None),
            P("section", None),
            P(),
            P("section", "dp"),
            P("section", "dp"),
        ),
        out_specs=(P("section", "dp", "seq", None), P("section", "dp", "seq", None)),
        check_vma=False,
    )
```
